32 devices in a mesh: req: 2 (over x), ctx: 4 (over y, core), tp: 4 (over z).
Axes of the slice: x: 2, y: 2, z: 4, core: 2. Of those that a mesh axis runs over, the one named last changes fastest.
Arguments:
- queries: bfloat16 [512, 16, 128], P('req', 'tp'), may hold values from -5 to 5
- new_keys: bfloat16 [512, 4, 128], P('req', 'tp'), may hold values from -5 to 5
- new_values: bfloat16 [512, 4, 128], P('req', 'tp'), may hold values from -24 to 24
- cache_keys: bfloat16 [2, 8192, 4, 128], P('req', 'ctx', 'tp'), may hold values from -5 to 5
- cache_values: bfloat16 [2, 8192, 4, 128], P('req', 'ctx', 'tp'), may hold values from -24 to 24
- cache_lengths: int32 [2], replicated, may hold values from 1 to 8192, as said below
- residual: bfloat16 [512, 2048], P(('req', 'ctx'), 'tp'), may hold values from -24 to 24
- out_weight: bfloat16 [2048, 2048], P('tp', 'ctx'), may hold values from -0.52734375 to 0.52734375
- norm_gain: float32 [2048], replicated, may hold values from 0.1 to 1.9
- expert_ids: int32 [512, 6], P(('req', 'ctx')), may hold values from 0 to 63, all different within a row; in each aligned block of 64 rows (0 to 63, 64 to 127, ...) at most 8 rows name the same one
- gate_weights: float32 [512, 6], P(('req', 'ctx')), may hold values from 0.1 to 1
- w_gate: bfloat16 [64, 2048, 1408], P('req', 'ctx', 'tp'), may hold values from -0.125 to 0.125
- w_up: bfloat16 [64, 2048, 1408], P('req', 'ctx', 'tp'), may hold values from -0.125 to 0.125
- w_down: bfloat16 [64, 1408, 2048], P('req', 'tp', 'ctx'), may hold values from -0.15625 to 0.15625
Outputs:
- layer_out: bfloat16 [512, 2048], P(('req', 'ctx'), 'tp')
The draws below stay inside these ranges and needn't reach their ends.
Inputs may be any that keep to these rules, and one draw needn't show every extreme that they name: `cache_lengths`: the longest cached length equals 8192. `expert_ids`: within each aligned block of 64 tokens no expert is named by more than 8 routes, a bound that some block reaches.
All inputs are finite; a program needn't handle non-finite values.
Results may differ from the reference program's by a relative error of at most 0.006.
Values may be sent and summed in bfloat16 or wider, within the bound.
A program may use at most 384 MiB of HBM per device.

```python
import math
import jax
import jax.numpy as jnp
import numpy as np
from jax import lax

D = 2048
H = 16
KVH = 4
HD = 128
FF = 1408
EXPERTS = 64
TOP = 6
TOK_DEV = 256
CTX_DEV = 2048
CAP = 8
REQS = 2
TOKENS = 512
CACHE = 8192
FF_DEV = 352
MOE_DEV = 64
N_CTX = 4
N_TP = 4


def draw_queries(key, part):
    noise_key = jax.random.fold_in(key, 1)
    base = jax.random.truncated_normal(noise_key, -4.0, 4.0, (TOKENS, H, HD), jnp.float32)
    return base.astype(jnp.bfloat16)


def draw_new_keys(key, part):
    noise_key = jax.random.fold_in(key, 2)
    base = jax.random.truncated_normal(noise_key, -4.0, 4.0, (TOKENS, KVH, HD), jnp.float32)
    return base.astype(jnp.bfloat16)


def draw_cache_keys(key, part):
    noise_key = jax.random.fold_in(key, 3)
    base = jax.random.truncated_normal(noise_key, -4.0, 4.0, (REQS, CACHE, KVH, HD), jnp.float32)
    return base.astype(jnp.bfloat16)


def draw_cache_lengths(key, part):
    others = jax.random.randint(jax.random.fold_in(key, 11), (REQS,), 1, CACHE, jnp.int32)
    longest = jax.random.randint(jax.random.fold_in(key, 12), (), 0, REQS, jnp.int32)
    chosen = jnp.arange(REQS, dtype=jnp.int32) == longest
    return jnp.where(chosen, jnp.int32(CACHE), others).astype(jnp.int32)


def draw_residual(key, part):
    row_scale = jnp.exp(jax.random.uniform(jax.random.fold_in(key, 4), (TOKENS, 1), jnp.float32, jnp.log(0.3), jnp.log(3.0)))
    column_scale = jnp.exp(jax.random.uniform(jax.random.fold_in(key, 5), (1, D), jnp.float32, jnp.log(0.5), jnp.log(2.0)))
    base = jax.random.truncated_normal(jax.random.fold_in(key, 8), -4.0, 4.0, (TOKENS, D), jnp.float32)
    return (base * row_scale * column_scale).astype(jnp.bfloat16)


def steps_of(key, shape, cuts, smallest, top_value):
    def one(axis_at, shards_of):
        draws = jax.random.uniform(jax.random.fold_in(jax.random.fold_in(key, 6), axis_at), (shards_of,), jnp.float32, smallest / len(cuts), top_value / len(cuts))
        return jnp.repeat(jnp.exp(draws), shape[axis_at] // shards_of).reshape((-1,) + (1,) * (len(shape) - axis_at - 1))

    loudness = one(*cuts[0])
    for cut in cuts[1:]:
        loudness = loudness * one(*cut)
    return loudness


def deal_out(own_key, own, number, rows, amount, top, reach, slope):
    ranking = jax.random.permutation(own_key, amount)
    crowded, ordinary = shares(amount, rows * top, reach, slope, True), shares(amount, rows * top, reach, slope, False)
    places = jnp.arange(amount)

    def named(lengths, rotation):
        used = int((lengths > 0).sum())
        fixed = max(1, used // 4)
        moved = fixed + (places - fixed + rotation * (used - fixed)) % max(1, amount - fixed)
        return jnp.zeros((amount,), jnp.int32).at[ranking[jnp.where(places < fixed, places, moved)]].set(jnp.asarray(lengths, jnp.int32))

    lengths = jnp.where(number % 4 == 0, named(crowded, number // 4), named(ordinary, number - number // 4 - 1))
    mixed = jax.random.permutation(jax.random.fold_in(own, 3), amount)
    donor, receiver = mixed[0:amount // 2 * 2:2], mixed[1:amount // 2 * 2:2]
    room = jnp.minimum(lengths[donor] - 1, reach - lengths[receiver]) // 2
    room = jnp.where((donor == ranking[0]) | (receiver == ranking[0]) | (lengths[receiver] == 0), 0, jnp.maximum(room, 0))
    moved = jax.random.randint(jax.random.fold_in(own, 4), (amount // 2,), 0, 1 << 20) % (room + 1)
    lengths = lengths.at[donor].add(-moved).at[receiver].add(moved)
    items = jnp.searchsorted(jnp.cumsum(lengths), jnp.arange(rows * top), side="right").astype(jnp.int32)
    grid = items.reshape(top, rows).T
    grid = grid[jax.random.permutation(jax.random.fold_in(own, 1), rows)]
    rotation = jax.random.randint(jax.random.fold_in(own, 2), (rows, 1), 0, top)
    return jnp.take_along_axis(grid, (jnp.arange(top)[None, :] + rotation) % top, axis=1)


def shares(amount, total, limit, lean, full):
    loads = [(1 << 20) // math.isqrt(grade ** lean) + 1 for grade in range(1, amount + 1)]
    largest = limit if full else min(limit, max(-(-total // amount), total * loads[0] // sum(loads)))
    least = 1 if total - largest >= amount - 1 else 0
    given, rest = [largest] + [least] * (amount - 1), total - largest - least * (amount - 1)
    while rest > 0:
        free = [i for i in range(1, amount) if given[i] < largest] or [i for i in range(1, amount) if given[i] < limit]
        pool, left = sum([loads[i] for i in free]), rest
        for i in free:
            more = min(limit - given[i], max(1, left * loads[i] // pool), rest)
            given[i] = given[i] + more
            rest = rest - more
    return np.array(given)


def scatter_about(stream_key, shape, spread, most, split=(), held_as=jnp.bfloat16):
    factor_of = steps_of(stream_key, shape, split, -0.22, 0.18) if split else 1.0
    drawn = jax.random.normal(stream_key, shape, jnp.float32) * spread * factor_of
    return jnp.minimum(jnp.maximum(drawn, -most), most).astype(held_as)


def setup_inputs(seed: int = 0) -> dict:
    arg_keys = jax.random.split(jax.random.key(seed), 15)
    queries = draw_queries(jax.random.fold_in(arg_keys[14], 71), 0)
    new_keys = draw_new_keys(jax.random.fold_in(arg_keys[14], 71), 0)
    new_values = scatter_about(arg_keys[2], (TOKENS, KVH, HD), 4.0, 24.0, ((0, 2), (1, 4)))
    cache_keys = draw_cache_keys(jax.random.fold_in(arg_keys[14], 71), 0)
    cache_values = scatter_about(arg_keys[4], (REQS, CACHE, KVH, HD), 4.0, 24.0, ((0, 2), (1, 4), (2, 4)))
    cache_lengths = draw_cache_lengths(jax.random.fold_in(arg_keys[14], 71), 0)
    residual = draw_residual(jax.random.fold_in(arg_keys[14], 71), 0)
    out_weight = scatter_about(arg_keys[7], (H * HD, D), (4.0 / (H * HD) ** 0.5), 0.52734375, ((0, 4), (1, 4)))
    norm_gain = jnp.clip(1.0 + 0.18 * jax.random.normal(arg_keys[8], (D,), jnp.float32), 0.1, 1.9)
    expert_ids_keys = jax.random.split(jax.random.fold_in(arg_keys[9], 1), TOKENS // MOE_DEV)
    expert_ids_turns = jax.random.permutation(jax.random.fold_in(arg_keys[9], 3), TOKENS // MOE_DEV)
    expert_ids = jax.vmap(lambda own, number: deal_out(jax.random.fold_in(arg_keys[9], 2), own, number, MOE_DEV, EXPERTS, TOP, CAP, 2))(expert_ids_keys, expert_ids_turns).reshape((TOKENS, TOP))
    gate_weights = jnp.clip(0.1 + 0.9 * jax.random.uniform(arg_keys[10], (TOKENS, TOP), jnp.float32) ** steps_of(arg_keys[10], (TOKENS, TOP), ((0, 8),), -0.2, 0.2), 0.1, 1.0)
    w_gate = scatter_about(arg_keys[11], (EXPERTS, D, FF), D ** -0.5, 0.125, ((0, 2), (1, 4), (2, 4)))
    w_up = scatter_about(arg_keys[12], (EXPERTS, D, FF), D ** -0.5, 0.125, ((0, 2), (1, 4), (2, 4)))
    w_down = scatter_about(arg_keys[13], (EXPERTS, FF, D), FF ** -0.5, 0.15625, ((0, 2), (1, 4), (2, 4)))
    return {"queries": queries, "new_keys": new_keys, "new_values": new_values, "cache_keys": cache_keys, "cache_values": cache_values, "cache_lengths": cache_lengths, "residual": residual, "out_weight": out_weight, "norm_gain": norm_gain, "expert_ids": expert_ids, "gate_weights": gate_weights, "w_gate": w_gate, "w_up": w_up, "w_down": w_down}


masked_score = -1e+30

def attend_request(request, queries, new_keys, new_values, cache_keys, cache_values, cache_lengths):
    scale = 1.0 / HD ** 0.5
    start = request * TOK_DEV
    query_rows = lax.dynamic_slice_in_dim(queries, start, TOK_DEV, 0)
    fresh_keys = lax.dynamic_slice_in_dim(new_keys, start, TOK_DEV, 0)
    fresh_values = lax.dynamic_slice_in_dim(new_values, start, TOK_DEV, 0)
    old_keys = lax.dynamic_index_in_dim(cache_keys, request, 0, keepdims=False)
    old_values = lax.dynamic_index_in_dim(cache_values, request, 0, keepdims=False)
    length = lax.dynamic_index_in_dim(cache_lengths, request, 0, keepdims=False)
    key_rows = jnp.concatenate([old_keys, fresh_keys], 0)
    cache_valid = (jnp.arange(CACHE, dtype=jnp.int32) < length).reshape(N_CTX, CTX_DEV)
    positions = jnp.arange(TOK_DEV, dtype=jnp.int32)
    causal = positions[None, :] <= positions[:, None]
    group_size = H // KVH
    pieces = []
    for group in range(KVH):
        grouped = query_rows[:, group * group_size:(group + 1) * group_size, :].reshape(TOK_DEV * group_size, HD)
        scores = jnp.dot(grouped, key_rows[:, group, :].T, preferred_element_type=jnp.float32) * scale
        scores = scores.reshape(TOK_DEV, group_size, CACHE + TOK_DEV)
        cached = scores[:, :, :CACHE].reshape(TOK_DEV, group_size, N_CTX, CTX_DEV)
        cached = jnp.where(cache_valid[None, None], cached, masked_score)
        fresh = jnp.where(causal[:, None, :], scores[:, :, CACHE:], masked_score)
        cached_max = lax.optimization_barrier(jnp.max(cached, -1))
        last_max = jnp.maximum(cached_max[:, :, -1], lax.optimization_barrier(jnp.max(fresh, -1)))
        block_max = jnp.concatenate([cached_max[:, :, :-1], last_max[:, :, None]], -1)
        cached_weights = jnp.where(cache_valid[None, None], jnp.exp(cached - block_max[..., None]), 0.0)
        fresh_weights = jnp.where(causal[:, None, :], jnp.exp(fresh - last_max[..., None]), 0.0)
        block_total = lax.optimization_barrier(jnp.sum(cached_weights, -1))
        block_total = block_total.at[:, :, -1].add(lax.optimization_barrier(jnp.sum(fresh_weights, -1)))
        cached_rounded_scores = lax.optimization_barrier(cached_weights.astype(jnp.bfloat16)).astype(jnp.float32)
        fresh_round = lax.optimization_barrier(fresh_weights.astype(jnp.bfloat16)).astype(jnp.float32)
        block_value_rows = old_values[:, group, :].reshape(N_CTX, CTX_DEV, HD).astype(jnp.float32)
        block_partial_sum = jnp.einsum('osqz,qzl->osql', cached_rounded_scores, block_value_rows, precision=lax.Precision.HIGHEST)
        fresh_sum = jnp.einsum('tgk,kd->tgd', fresh_round, fresh_values[:, group, :].astype(jnp.float32), precision=lax.Precision.HIGHEST)
        block_partial_sum = block_partial_sum.at[:, :, -1].add(fresh_sum)
        top = lax.optimization_barrier(jnp.max(block_max, -1, keepdims=True))
        factor = jnp.exp(block_max - top)
        total = lax.optimization_barrier(jnp.sum(factor * block_total, -1))
        weighted = lax.optimization_barrier(jnp.sum(factor[..., None] * block_partial_sum, 2))
        pieces.append(weighted / total[..., None])
    return jnp.concatenate(pieces, 1).reshape(TOK_DEV, H * HD).astype(jnp.bfloat16)

def reference(queries, new_keys, new_values, cache_keys, cache_values, cache_lengths, residual, out_weight, norm_gain, expert_ids, gate_weights, w_gate, w_up, w_down):

    def one_request(request):
        return attend_request(request, queries, new_keys, new_values, cache_keys, cache_values, cache_lengths)
    attention_result = lax.map(one_request, jnp.arange(REQS, dtype=jnp.int32)).reshape(TOKENS, H * HD)
    hidden = residual.astype(jnp.float32) + jnp.dot(attention_result, out_weight, preferred_element_type=jnp.float32)
    mean_square = lax.optimization_barrier(jnp.mean(hidden * hidden, -1, keepdims=True))
    normed = (hidden * lax.rsqrt(mean_square + 1e-06) * norm_gain).astype(jnp.bfloat16)
    flat_ids = expert_ids.reshape(-1)
    flat_gates = gate_weights.reshape(-1)
    flat_tokens = (jnp.arange(TOKENS * TOP, dtype=jnp.int32) // TOP).astype(jnp.int32)
    slot_limit = CAP * (TOKENS // MOE_DEV)

    def expert_step(accum_sum, expert):
        matches = flat_ids == expert
        count = jnp.sum(matches.astype(jnp.int32))
        picked_rows = jnp.nonzero(matches, size=slot_limit, fill_value=0)[0].astype(jnp.int32)
        is_live = jnp.arange(slot_limit, dtype=jnp.int32) < count
        token_ids = flat_tokens[picked_rows]
        factors = jnp.where(is_live, flat_gates[picked_rows], 0.0)
        gathered = normed[token_ids]
        gate_act = jnp.dot(gathered, w_gate[expert], preferred_element_type=jnp.float32)
        up_act = jnp.dot(gathered, w_up[expert], preferred_element_type=jnp.float32)
        inner = (jax.nn.silu(gate_act) * up_act).astype(jnp.bfloat16)
        down_rows = w_down[expert]
        routed_tokens = jnp.zeros((slot_limit, D), jnp.float32)
        for group in range(N_TP):
            piece_out = jnp.dot(inner[:, group * FF_DEV:(group + 1) * FF_DEV], down_rows[group * FF_DEV:(group + 1) * FF_DEV, :], preferred_element_type=jnp.float32)
            routed_tokens = routed_tokens + piece_out.astype(jnp.bfloat16).astype(jnp.float32)
        accum_sum = accum_sum.at[token_ids].add(factors[:, None] * routed_tokens)
        return (accum_sum, None)
    expert_mixture, unused = lax.scan(expert_step, jnp.zeros((TOKENS, D), jnp.float32), jnp.arange(EXPERTS, dtype=jnp.int32))
    return (hidden + expert_mixture).astype(jnp.bfloat16)
```

```python
import jax
import jax.numpy as jnp
from jax import lax
from jax.sharding import PartitionSpec as P

TOP = 6
CAP = 8
MASKED = -1e30


def attention_part(queries, new_keys, new_values, cache_keys, cache_values, length):
    ctx_pos, ctx_count = lax.axis_index("ctx"), lax.axis_size("ctx")
    tok_dev, heads, hd = queries.shape
    cache_dev = cache_keys.shape[1]
    block = tok_dev // ctx_count
    rows = heads * block
    q = queries.reshape(ctx_count, block, heads, hd).transpose(0, 2, 1, 3)
    q = q.reshape(ctx_count * rows, hd)
    keys = jnp.concatenate([cache_keys[0, :, 0, :], new_keys[:, 0, :]], 0)
    values = jnp.concatenate([cache_values[0, :, 0, :], new_values[:, 0, :]], 0)
    scores = jnp.dot(keys, q.T, preferred_element_type=jnp.float32) * (hd**-0.5)
    key_at = jnp.arange(cache_dev + tok_dev, dtype=jnp.int32)[:, None]
    row_at = jnp.arange(ctx_count * rows, dtype=jnp.int32)[None, :]
    token = (row_at // rows) * block + row_at % block
    valid = jnp.where(
        key_at < cache_dev,
        ctx_pos * cache_dev + key_at < length,
        jnp.logical_and(ctx_pos == ctx_count - 1, key_at - cache_dev <= token),
    )
    scores = jnp.where(valid, scores, MASKED)
    top = jnp.max(scores, 0, keepdims=True)
    weights = jnp.where(valid, jnp.exp(scores - top), 0.0)
    total = jnp.sum(weights, 0, keepdims=True)
    sums = lax.dot_general(
        values,
        weights.astype(jnp.bfloat16),
        (((0,), (0,)), ((), ())),
        preferred_element_type=jnp.float32,
    )
    pack = jnp.concatenate([sums, top, total, jnp.zeros((6, ctx_count * rows), jnp.float32)], 0)
    return pack.reshape(hd + 8, ctx_count, rows).transpose(1, 0, 2)


def merge(packs, hd, heads):
    top = jnp.max(packs[:, hd : hd + 1], 0)
    factor = jnp.exp(packs[:, hd : hd + 1] - top)
    total = jnp.sum(factor * packs[:, hd + 1 : hd + 2], 0)
    out = (jnp.sum(factor * packs[:, :hd], 0) / total).astype(jnp.bfloat16)
    block = out.shape[1] // heads
    return out.reshape(hd, heads, block).transpose(2, 1, 0).reshape(block, heads * hd)


def route_tables(expert_ids, gate_weights, exp_dev):
    block = expert_ids.shape[0]
    both = jnp.concatenate([expert_ids.astype(jnp.float32), gate_weights], 1)
    both = lax.all_gather(both, ("req", "ctx"))
    blocks = both.shape[0]
    ids = both[:, :, :TOP].astype(jnp.int32)
    gates = both[:, :, TOP:]
    first = lax.axis_index("req") * exp_dev
    experts = first + jnp.arange(exp_dev, dtype=jnp.int32)
    hits = ids[:, :, :, None] == experts
    gate_at = jnp.sum(jnp.where(hits, gates[..., None], 0.0), 2)
    hit = jnp.any(hits, 2)
    earlier = jnp.tril(jnp.ones((block, block), jnp.bfloat16), -1)
    rank = jnp.einsum(
        "ij,bje->bie", earlier, hit.astype(jnp.bfloat16), preferred_element_type=jnp.float32
    )
    code = jnp.arange(blocks, dtype=jnp.int32)[:, None, None] * CAP + rank.astype(jnp.int32)
    code = jnp.where(hit, code, -1)
    flat = (blocks * block, exp_dev)
    return code.reshape(flat).T, gate_at.reshape(flat).T


def body(
    queries,
    new_keys,
    new_values,
    cache_keys,
    cache_values,
    cache_lengths,
    residual,
    out_weight,
    norm_gain,
    expert_ids,
    gate_weights,
    w_gate,
    w_up,
    w_down,
):
    ctx_pos, tp_pos, req_pos = (lax.axis_index(a) for a in ("ctx", "tp", "req"))
    ctx_count, req_count = lax.axis_size("ctx"), lax.axis_size("req")
    tok_dev, heads, hd = queries.shape
    block, share = residual.shape
    exp_dev = w_gate.shape[0]
    slots = req_count * ctx_count * CAP
    length = lax.dynamic_index_in_dim(cache_lengths, req_pos, 0, keepdims=False)
    code, gate_at = route_tables(expert_ids, gate_weights, exp_dev)
    swap = [(a * ctx_count + b, b * ctx_count + a) for a in range(ctx_count) for b in range(ctx_count)]
    residual_t = lax.ppermute(residual, ("ctx", "tp"), swap)
    packs = attention_part(queries, new_keys, new_values, cache_keys, cache_values, length)
    packs = lax.all_to_all(packs, "ctx", 0, 0, tiled=True)
    attended = merge(packs, hd, heads)
    attended = lax.all_gather(attended, "ctx", tiled=True)
    part = jnp.dot(attended, out_weight, preferred_element_type=jnp.float32)
    part = part.reshape(-1, block, share)
    part = lax.all_to_all(part, "tp", 0, 0, tiled=True)
    hidden = jnp.sum(part, 0) + residual_t.astype(jnp.float32)
    squares = jnp.sum(hidden * hidden, 1)
    gain = lax.dynamic_slice_in_dim(norm_gain, ctx_pos * share, share, 0)
    scaled = (hidden * gain).astype(jnp.bfloat16)
    squares = lax.psum(squares, "ctx")
    factor = lax.rsqrt(squares / norm_gain.shape[0] + 1e-6)
    factor = lax.all_gather(factor, ("req", "tp"), tiled=True)
    scaled = lax.all_gather(scaled, ("req", "tp"), tiled=True)
    pick = code[:, None, :] == jnp.arange(slots, dtype=jnp.int32)[None, :, None]
    row_factor = jnp.sum(jnp.where(pick, factor, 0.0), -1, keepdims=True)
    row_gate = jnp.sum(jnp.where(pick, gate_at[:, None, :], 0.0), -1, keepdims=True)
    pick = pick.astype(jnp.bfloat16)
    rows = jnp.einsum("est,td->esd", pick, scaled, preferred_element_type=jnp.bfloat16)
    gate = jnp.einsum("esd,edf->esf", rows, w_gate, preferred_element_type=jnp.float32)
    up = jnp.einsum("esd,edf->esf", rows, w_up, preferred_element_type=jnp.float32)
    both = jnp.stack([gate, up], 2).astype(jnp.bfloat16)
    both = both.reshape(ctx_count, exp_dev * slots // ctx_count, 2, -1)
    both = lax.all_to_all(both, "ctx", 0, 0, tiled=True)
    both = both.astype(jnp.float32).sum(0)
    per = exp_dev * slots // ctx_count
    mine = lax.dynamic_slice_in_dim(row_factor.reshape(-1, 1), ctx_pos * per, per, 0)
    inner = (jax.nn.silu(both[:, 0] * mine) * (both[:, 1] * mine)).astype(jnp.bfloat16)
    inner = lax.all_gather(inner, "ctx", tiled=True).reshape(exp_dev, slots, -1)
    down = jnp.einsum("esf,efd->esd", inner, w_down, preferred_element_type=jnp.float32)
    down = (down * row_gate).astype(jnp.bfloat16)
    mixed = jnp.einsum("est,esd->td", pick, down, preferred_element_type=jnp.float32)
    mixed = mixed.astype(jnp.bfloat16).reshape(-1, block, share)
    mixed = lax.all_to_all(mixed, ("req", "tp"), 0, 0, tiled=True)
    out = hidden + jnp.sum(mixed.astype(jnp.float32), 0)
    return lax.ppermute(out.astype(jnp.bfloat16), ("ctx", "tp"), swap)


def solution(mesh):
    in_specs = (
        P("req", "tp", None),
        P("req", "tp", None),
        P("req", "tp", None),
        P("req", "ctx", "tp", None),
        P("req", "ctx", "tp", None),
        P(),
        P(("req", "ctx"), "tp"),
        P("tp", "ctx"),
        P(),
        P(("req", "ctx"), None),
        P(("req", "ctx"), None),
        P("req", "ctx", "tp"),
        P("req", "ctx", "tp"),
        P("req", "tp", "ctx"),
    )
    out_specs = P(("req", "ctx"), "tp")
    return jax.shard_map(body, mesh=mesh, in_specs=in_specs, out_specs=out_specs, check_vma=False)
```

```python
import functools
import jax
import jax.numpy as jnp
from jax import lax
from jax.experimental import pallas as pl
from jax.experimental.pallas import tpu as pltpu
from jax.sharding import PartitionSpec as P

TOP = 6
CAP = 8
MASKED = -1e30
F32 = jnp.float32
BF16 = jnp.bfloat16
CHUNKS = 4
FUSED_BYTES = 4 * 1024 * 1024


def dot(a, b, contract, kind=F32):
    return lax.dot_general(a, b, (contract, ((), ())), preferred_element_type=kind)


def layer_kernel(
    dims,
    len_ref,
    q_ref,
    ck_ref,
    cv_ref,
    nk_ref,
    nv_ref,
    res_ref,
    ow_ref,
    gain_ref,
    rt_ref,
    wg_hbm,
    wu_hbm,
    wd_hbm,
    out_ref,
    wg,
    wu,
    wd,
    pk_send,
    pk_recv,
    att,
    part,
    part_recv,
    res_t,
    hidden,
    sq,
    fac,
    tab,
    codes,
    tok,
    pick,
    x,
    gu,
    r1,
    s2,
    r2,
    inner,
    ys,
    acc,
    mix,
    mix_recv,
    tsend,
    trecv,
    fin,
    fin_recv,
    w_sem,
    ssem,
    rsem,
):
    reqs, ctxs, tps, block, heads, hd, exp_dev, slots, ff, share = dims
    r, c, t = lax.axis_index("req"), lax.axis_index("ctx"), lax.axis_index("tp")
    blocks = reqs * ctxs
    tokens = blocks * block
    chunk = exp_dev * slots // CHUNKS
    quarter = chunk // ctxs
    rb = min(slots, quarter)
    y, k = c // 2, c % 2
    count = [0]

    def rcopy(src, dst, **where):
        i = count[0]
        count[0] = i + 1
        return pltpu.make_async_remote_copy(
            src_ref=src,
            dst_ref=dst,
            send_sem=ssem.at[i],
            recv_sem=rsem.at[i],
            device_id={"req": r, "ctx": c, "tp": t} | where,
            device_id_type=pl.DeviceIdType.MESH,
        )

    def step(me, d, n):
        return lax.rem(me + d, n)

    loads = [
        pltpu.make_async_copy(wg_hbm, wg, w_sem.at[0]),
        pltpu.make_async_copy(wu_hbm, wu, w_sem.at[1]),
        pltpu.make_async_copy(wd_hbm, wd, w_sem.at[2]),
    ]
    for load in loads:
        load.start()

    barrier = pltpu.get_barrier_semaphore()
    peers = [
        {"req": step(r, a, reqs), "ctx": step(c, b, ctxs), "tp": t}
        for a in range(reqs)
        for b in range(ctxs)
        if a or b
    ] + [{"req": r, "ctx": c, "tp": step(t, d, tps)} for d in range(1, tps)]
    swap = {"ctx": t, "tp": c}
    for peer in peers:
        pl.semaphore_signal(barrier, 1, device_id=peer, device_id_type=pl.DeviceIdType.MESH)

    @pl.when(c != t)
    def _():
        pl.semaphore_signal(
            barrier, 1, device_id={"req": r} | swap, device_id_type=pl.DeviceIdType.MESH
        )
        pl.semaphore_wait(barrier, len(peers) + 1)

    @pl.when(c == t)
    def _():
        pl.semaphore_wait(barrier, len(peers))

    pending = []

    me = r * ctxs + c
    tab_copies = []
    for a in range(reqs):
        for b in range(ctxs):
            if a or b:
                to = step(r, a, reqs)
                copy = rcopy(rt_ref.at[to], tab.at[me], req=to, ctx=step(c, b, ctxs))
                copy.start()
                tab_copies.append(copy)
    tab[me] = rt_ref[r]
    res_copy = rcopy(res_ref, res_t, **swap)

    @pl.when(c != t)
    def _():
        res_copy.start()

    @pl.when(c == t)
    def _():
        res_t[...] = res_ref[...]

    length = len_ref[r]
    cache_dev, new_dev = ck_ref.shape[0], nk_ref.shape[0]
    rows = heads * block
    scale = hd**-0.5
    old_at = lax.broadcasted_iota(jnp.int32, (cache_dev, rows), 0)
    old_ok = old_at < length - c * cache_dev
    new_at = lax.broadcasted_iota(jnp.int32, (new_dev, rows), 0)
    lane = lax.broadcasted_iota(jnp.int32, (new_dev, rows), 1) % block
    stat_at = lax.broadcasted_iota(jnp.int32, (8, rows), 0)
    last = jnp.where(c == ctxs - 1, 0, new_dev)
    pk_copies = []
    for d in list(range(1, ctxs)) + [0]:
        b = step(c, d, ctxs)
        q = q_ref[b]
        new_ok = new_at + last <= lane + b * block
        old = jnp.where(old_ok, dot(ck_ref[...], q, ((1,), (1,))) * scale, MASKED)
        new = jnp.where(new_ok, dot(nk_ref[...], q, ((1,), (1,))) * scale, MASKED)
        top = jnp.maximum(
            jnp.max(old, 0, keepdims=True), jnp.max(new, 0, keepdims=True)
        )
        old = jnp.where(old_ok, jnp.exp(old - top), 0.0)
        new = jnp.where(new_ok, jnp.exp(new - top), 0.0)
        total = jnp.sum(old, 0, keepdims=True) + jnp.sum(new, 0, keepdims=True)
        sums = dot(cv_ref[...], old.astype(BF16), ((0,), (0,)))
        sums = sums + dot(nv_ref[...], new.astype(BF16), ((0,), (0,)))
        pk_send[d, 0:hd, :] = sums
        pk_send[d, hd : hd + 8, :] = jnp.where(
            stat_at == 0, top, jnp.where(stat_at == 1, total, 0.0)
        )
        if d:
            copy = rcopy(pk_send.at[d], pk_recv.at[d], ctx=b)
            copy.start()
            pk_copies.append(copy)
    for copy in pk_copies:
        copy.wait_recv()
    pending += pk_copies
    packs = [pk_send.at[0]] + [pk_recv.at[d] for d in range(1, ctxs)]
    tops = [p[hd : hd + 1, :] for p in packs]
    top = functools.reduce(jnp.maximum, tops)
    total = jnp.zeros((1, rows), F32)
    sums = jnp.zeros((hd, rows), F32)
    for p, own in zip(packs, tops):
        factor = jnp.exp(own - top)
        total = total + factor * p[hd + 1 : hd + 2, :]
        sums = sums + factor * p[0:hd, :]
    out = jnp.transpose(sums / total)
    for h in range(heads):
        att[c, :, h * hd : (h + 1) * hd] = out[h * block : (h + 1) * block].astype(BF16)
    att_copies = []
    for d in range(1, ctxs):
        copy = rcopy(att.at[c], att.at[c], ctx=step(c, d, ctxs))
        copy.start()
        att_copies.append(copy)
    for copy in tab_copies:
        copy.wait_recv()
    pending += tab_copies
    for p in range(blocks // 2):
        codes[:, p * 128 : (p + 1) * 128] = tab[2 * p] + tab[2 * p + 1]
    slot_at = lax.broadcasted_iota(jnp.int32, (rb, tokens), 0).astype(F32)

    def make_pick(i, carry):
        row = i * rb
        e = row // slots
        code = codes[pl.ds(e, 1), :] - (row - e * slots + 1).astype(F32)
        pick[pl.ds(pl.multiple_of(row, rb), rb), :] = jnp.where(
            slot_at == code, 1.0, 0.0
        ).astype(BF16)
        return carry

    lax.fori_loop(0, exp_dev * slots // rb, make_pick, 0)
    for copy in att_copies:
        copy.wait_recv()
    pending += att_copies
    width = heads * hd
    full = dot(att[...].reshape(ctxs * block, width), ow_ref[...], ((1,), (0,)))
    part[...] = full.reshape(tps, block, share)
    part_copies = []
    for d in range(1, tps):
        to = step(t, d, tps)
        copy = rcopy(part.at[to], part_recv.at[d], tp=to)
        copy.start()
        part_copies.append(copy)
    hid = part[t]

    @pl.when(c != t)
    def _():
        res_copy.wait_recv()

    hid = hid + res_t[...].astype(F32)
    for d in range(1, tps):
        part_copies[d - 1].wait_recv()
        hid = hid + part_recv[d]
    pending += part_copies
    hidden[...] = hid
    tok[r * tps + t] = (hid * gain_ref[...]).astype(BF16)
    tok_copies = []
    for a in range(reqs):
        for d in range(tps):
            if (a == 0) and d:
                copy = rcopy(tok.at[r * tps + t], tok.at[r * tps + t], tp=step(t, d, tps))
                copy.start()
                tok_copies.append(copy)
    far_copies = []
    for a in range(1, reqs):
        copy = rcopy(tok.at[r * tps + t], tok.at[r * tps + t], req=step(r, a, reqs))
        copy.start()
        far_copies.append(copy)
    sq[0] = jnp.broadcast_to(jnp.sum(hid * hid, 1, keepdims=True), (block, 128))
    sq_copies = []
    for d in range(1, ctxs):
        copy = rcopy(sq.at[0], sq.at[d], ctx=step(c, d, ctxs))
        copy.start()
        sq_copies.append(copy)
    for copy in sq_copies:
        copy.wait_recv()
    pending += sq_copies
    squares = sq[0]
    for d in range(1, ctxs):
        squares = squares + sq[d]
    fac[r * tps + t] = lax.rsqrt(squares / (share * ctxs) + 1e-6)
    fac_copies = []
    for d in range(1, tps):
        copy = rcopy(fac.at[r * tps + t], fac.at[r * tps + t], tp=step(t, d, tps))
        copy.start()
        fac_copies.append(copy)
    fac_far = []
    for a in range(1, reqs):
        copy = rcopy(fac.at[r * tps + t], fac.at[r * tps + t], req=step(r, a, reqs))
        copy.start()
        fac_far.append(copy)
    for d in range(1, tps):
        tok_copies[d - 1].wait_recv()
        at = r * tps + step(t, tps - d, tps)
        for a in range(1, reqs):
            copy = rcopy(tok.at[at], tok.at[at], req=step(r, a, reqs))
            copy.start()
            far_copies.append(copy)
    for d in range(1, tps):
        fac_copies[d - 1].wait_recv()
        at = r * tps + step(t, tps - d, tps)
        for a in range(1, reqs):
            copy = rcopy(fac.at[at], fac.at[at], req=step(r, a, reqs))
            copy.start()
            fac_far.append(copy)
    for copy in far_copies:
        copy.wait_recv()
    pending += tok_copies + far_copies + fac_copies
    loads[0].wait()
    loads[1].wait()

    n_sub = chunk // rb
    n_q = quarter // rb
    first, second, third, fourth = [], [], [], []

    def up_stage(j):
        base = j * chunk
        x[...] = dot(
            pick[base : base + chunk, :], tok[...].reshape(tokens, share), ((1,), (0,))
        ).astype(BF16)

        def one(i, carry):
            e = (base + i * rb) // slots
            at = pl.ds(pl.multiple_of((i % n_q) * rb, rb), rb)
            xs = x[pl.ds(pl.multiple_of(i * rb, rb), rb), :]
            q = i // n_q
            gu[0, j, q // 2, q % 2, at, :] = dot(xs, wg[e], ((1,), (0,))).astype(BF16)
            gu[1, j, q // 2, q % 2, at, :] = dot(xs, wu[e], ((1,), (0,))).astype(BF16)
            return carry

        lax.fori_loop(0, n_sub, one, 0)
        copy = rcopy(gu.at[:, j, :, 1 - k], r1.at[:, j], ctx=y * 2 + 1 - k)
        copy.start()
        first.append(copy)

    def pair_stage(j):
        first[j].wait_recv()
        s2[:, j] = (
            gu[:, j, 1 - y, k].astype(F32) + r1[:, j, 1 - y].astype(F32)
        ).astype(BF16)
        copy = rcopy(s2.at[:, j], r2.at[:, j], ctx=(1 - y) * 2 + k)
        copy.start()
        second.append(copy)

    def act_stage(j):
        second[j].wait_recv()
        both = gu[:, j, y, k].astype(F32) + r1[:, j, y].astype(F32) + r2[:, j].astype(F32)
        col = lax.broadcasted_iota(jnp.int32, (tokens, 128), 1)
        f = fac[...].reshape(tokens, 128)
        hi = f.astype(BF16).astype(F32)
        mid = (f - hi).astype(BF16).astype(F32)
        low = f - hi - mid
        f = jnp.where(col == 0, hi, jnp.where(col == 1, mid, jnp.where(col == 2, low, 0.0)))
        mine = pick[pl.ds(pl.multiple_of(j * chunk + c * quarter, quarter), quarter), :]
        row = jnp.sum(dot(mine, f.astype(BF16), ((1,), (0,))), 1, keepdims=True)
        g = both[0] * row
        inner[j, y, k] = (g * jax.nn.sigmoid(g) * (both[1] * row)).astype(BF16)
        copy = rcopy(inner.at[j, y, k], inner.at[j, y, k], ctx=(1 - y) * 2 + k)
        copy.start()
        third.append(copy)

    def share_stage(j):
        third[j].wait_recv()
        copy = rcopy(inner.at[j, :, k], inner.at[j, :, k], ctx=y * 2 + 1 - k)
        copy.start()
        fourth.append(copy)

    def down_stage(j):
        fourth[j].wait_recv()
        base = j * chunk

        def one(i, carry):
            e = (base + i * rb) // slots
            q = i // n_q
            at = pl.ds(pl.multiple_of((i % n_q) * rb, rb), rb)
            rows_at = pl.multiple_of(i * rb, rb)
            down = dot(inner[j, q // 2, q % 2, at, :], wd[e], ((1,), (0,)))
            mask = pick[pl.ds(pl.multiple_of(base + rows_at, rb), rb), :].astype(F32)
            gate = jnp.sum(mask * codes[pl.ds(exp_dev + e, 1), :], 1, keepdims=True)
            ys[pl.ds(rows_at, rb), :] = (down * gate).astype(BF16)
            return carry

        lax.fori_loop(0, n_sub, one, 0)
        term = dot(pick[base : base + chunk, :], ys[...], ((0,), (0,)))
        if j == 0:
            acc[...] = term
        else:
            acc[...] += term

    up_stage(0)
    up_stage(1)
    pair_stage(0)
    up_stage(2)
    for copy in fac_far:
        copy.wait_recv()
    pending.extend(fac_far)
    act_stage(0)
    pair_stage(1)
    up_stage(3)
    loads[2].wait()
    share_stage(0)
    act_stage(1)
    pair_stage(2)
    down_stage(0)
    share_stage(1)
    act_stage(2)
    pair_stage(3)
    down_stage(1)
    share_stage(2)
    act_stage(3)
    down_stage(2)
    share_stage(3)
    down_stage(3)
    pending += first + second + third + fourth

    per = tps * block
    mix_copies = []
    for a in range(1, reqs):
        to = step(r, a, reqs)
        mix[a] = acc[pl.ds(pl.multiple_of(to * per, per), per), :].astype(BF16)
        copy = rcopy(mix.at[a], mix_recv.at[a], req=to)
        copy.start()
        mix_copies.append(copy)
    mixed = acc[pl.ds(pl.multiple_of(r * per, per), per), :]
    for a in range(1, reqs):
        mix_copies[a - 1].wait_recv()
        mixed = mixed + mix_recv[a].astype(F32)
    pending += mix_copies
    tsend[...] = mixed.reshape(tps, block, share).astype(BF16)
    t_copies = []
    for d in range(1, tps):
        to = step(t, d, tps)
        copy = rcopy(tsend.at[to], trecv.at[d], tp=to)
        copy.start()
        t_copies.append(copy)
    total = hidden[...] + tsend[t].astype(F32)
    for d in range(1, tps):
        t_copies[d - 1].wait_recv()
        total = total + trecv[d].astype(F32)
    pending += t_copies
    fin[...] = total.astype(BF16)
    fin_copy = rcopy(fin, fin_recv, **swap)

    @pl.when(c != t)
    def _():
        fin_copy.start()
        fin_copy.wait()
        res_copy.wait_send()
        out_ref[...] = fin_recv[...]

    @pl.when(c == t)
    def _():
        out_ref[...] = fin[...]

    for copy in pending:
        copy.wait_send()


def fused_body(
    queries,
    new_keys,
    new_values,
    cache_keys,
    cache_values,
    cache_lengths,
    residual,
    out_weight,
    norm_gain,
    expert_ids,
    gate_weights,
    w_gate,
    w_up,
    w_down,
):
    reqs, ctxs, tps = (lax.axis_size(a) for a in ("req", "ctx", "tp"))
    r, c = lax.axis_index("req"), lax.axis_index("ctx")
    tok_dev, heads, hd = queries.shape
    block, share = residual.shape
    exp_dev, _, ff = w_gate.shape
    blocks = reqs * ctxs
    slots = blocks * CAP
    tokens = blocks * block
    chunk = exp_dev * slots // CHUNKS
    quarter = chunk // ctxs
    rows = heads * block
    q = queries.reshape(ctxs, block, heads, hd).transpose(0, 2, 1, 3).reshape(ctxs, rows, hd)
    me = r * ctxs + c
    experts = jnp.arange(reqs * exp_dev, dtype=jnp.int32)
    hits = expert_ids[None, :, :] == experts[:, None, None]
    gates = jnp.sum(jnp.where(hits, gate_weights[None], 0.0), 2)
    hit = jnp.any(hits, 2)
    later = jnp.triu(jnp.ones((block, block), BF16), 0)
    rank = jnp.dot(hit.astype(BF16), later, preferred_element_type=F32)
    code = jnp.where(hit, rank + (me * CAP).astype(F32), 0.0)
    table = jnp.stack([code.reshape(reqs, exp_dev, block), gates.reshape(reqs, exp_dev, block)], 1)
    table = table.reshape(reqs, 2 * exp_dev, block)
    zero = jnp.zeros_like(table)
    odd = me % 2 == 1
    table = jnp.concatenate([jnp.where(odd, zero, table), jnp.where(odd, table, zero)], 2)
    gain = lax.dynamic_slice_in_dim(norm_gain, c * share, share, 0).reshape(1, share)
    dims = (reqs, ctxs, tps, block, heads, hd, exp_dev, slots, ff, share)
    n_rem = (
        (blocks - 1)
        + 2
        + 2 * (ctxs - 1)
        + (tps - 1)
        + (ctxs - 1)
        + 2 * (tps - 1)
        + 2 * tps * (reqs - 1)
        + 4 * CHUNKS
        + (reqs - 1)
        + (tps - 1)
    )
    vmem = pl.BlockSpec(memory_space=pltpu.VMEM)
    anywhere = pl.BlockSpec(memory_space=pl.ANY)
    scratch = [
        ((exp_dev, share, ff), BF16),
        ((exp_dev, share, ff), BF16),
        ((exp_dev, ff, share), BF16),
        ((ctxs, hd + 8, rows), F32),
        ((ctxs, hd + 8, rows), F32),
        ((ctxs, block, heads * hd), BF16),
        ((tps, block, share), F32),
        ((tps, block, share), F32),
        ((block, share), BF16),
        ((block, share), F32),
        ((ctxs, block, 128), F32),
        ((reqs * tps, block, 128), F32),
        ((blocks, 2 * exp_dev, 128), F32),
        ((2 * exp_dev, tokens), F32),
        ((reqs * tps, block, share), BF16),
        ((exp_dev * slots, tokens), BF16),
        ((chunk, share), BF16),
        ((2, CHUNKS, 2, 2, quarter, ff), BF16),
        ((2, CHUNKS, 2, quarter, ff), BF16),
        ((2, CHUNKS, quarter, ff), BF16),
        ((2, CHUNKS, quarter, ff), BF16),
        ((CHUNKS, 2, 2, quarter, ff), BF16),
        ((chunk, share), BF16),
        ((tokens, share), F32),
        ((reqs, tps * block, share), BF16),
        ((reqs, tps * block, share), BF16),
        ((tps, block, share), BF16),
        ((tps, block, share), BF16),
        ((block, share), BF16),
        ((block, share), BF16),
    ]
    return pl.pallas_call(
        functools.partial(layer_kernel, dims),
        out_shape=jax.ShapeDtypeStruct((block, share), BF16),
        in_specs=[pl.BlockSpec(memory_space=pltpu.SMEM)] + [vmem] * 9 + [anywhere] * 3,
        out_specs=vmem,
        scratch_shapes=[pltpu.VMEM(*s) for s in scratch]
        + [
            pltpu.SemaphoreType.DMA((3,)),
            pltpu.SemaphoreType.DMA((n_rem,)),
            pltpu.SemaphoreType.DMA((n_rem,)),
        ],
        compiler_params=pltpu.CompilerParams(
            collective_id=0, has_side_effects=True, vmem_limit_bytes=63 * 1024 * 1024
        ),
    )(
        cache_lengths,
        q,
        cache_keys[0, :, 0, :],
        cache_values[0, :, 0, :],
        new_keys[:, 0, :],
        new_values[:, 0, :],
        residual,
        out_weight,
        gain,
        table,
        w_gate,
        w_up,
        w_down,
    )


def attention_part(queries, new_keys, new_values, cache_keys, cache_values, length):
    ctx_pos, ctx_count = lax.axis_index("ctx"), lax.axis_size("ctx")
    tok_dev, heads, hd = queries.shape
    cache_dev = cache_keys.shape[1]
    block = tok_dev // ctx_count
    rows = heads * block
    q = queries.reshape(ctx_count, block, heads, hd).transpose(0, 2, 1, 3)
    q = q.reshape(ctx_count * rows, hd)
    keys = jnp.concatenate([cache_keys[0, :, 0, :], new_keys[:, 0, :]], 0)
    values = jnp.concatenate([cache_values[0, :, 0, :], new_values[:, 0, :]], 0)
    scores = jnp.dot(keys, q.T, preferred_element_type=jnp.float32) * (hd**-0.5)
    key_at = jnp.arange(cache_dev + tok_dev, dtype=jnp.int32)[:, None]
    row_at = jnp.arange(ctx_count * rows, dtype=jnp.int32)[None, :]
    token = (row_at // rows) * block + row_at % block
    valid = jnp.where(
        key_at < cache_dev,
        ctx_pos * cache_dev + key_at < length,
        jnp.logical_and(ctx_pos == ctx_count - 1, key_at - cache_dev <= token),
    )
    scores = jnp.where(valid, scores, MASKED)
    top = jnp.max(scores, 0, keepdims=True)
    weights = jnp.where(valid, jnp.exp(scores - top), 0.0)
    total = jnp.sum(weights, 0, keepdims=True)
    sums = lax.dot_general(
        values,
        weights.astype(jnp.bfloat16),
        (((0,), (0,)), ((), ())),
        preferred_element_type=jnp.float32,
    )
    pack = jnp.concatenate([sums, top, total, jnp.zeros((6, ctx_count * rows), jnp.float32)], 0)
    return pack.reshape(hd + 8, ctx_count, rows).transpose(1, 0, 2)


def merge(packs, hd, heads):
    top = jnp.max(packs[:, hd : hd + 1], 0)
    factor = jnp.exp(packs[:, hd : hd + 1] - top)
    total = jnp.sum(factor * packs[:, hd + 1 : hd + 2], 0)
    out = (jnp.sum(factor * packs[:, :hd], 0) / total).astype(jnp.bfloat16)
    block = out.shape[1] // heads
    return out.reshape(hd, heads, block).transpose(2, 1, 0).reshape(block, heads * hd)


def route_tables(expert_ids, gate_weights, exp_dev):
    block = expert_ids.shape[0]
    both = jnp.concatenate([expert_ids.astype(jnp.float32), gate_weights], 1)
    both = lax.all_gather(both, ("req", "ctx"))
    blocks = both.shape[0]
    ids = both[:, :, :TOP].astype(jnp.int32)
    gates = both[:, :, TOP:]
    first = lax.axis_index("req") * exp_dev
    experts = first + jnp.arange(exp_dev, dtype=jnp.int32)
    hits = ids[:, :, :, None] == experts
    gate_at = jnp.sum(jnp.where(hits, gates[..., None], 0.0), 2)
    hit = jnp.any(hits, 2)
    earlier = jnp.tril(jnp.ones((block, block), jnp.bfloat16), -1)
    rank = jnp.einsum(
        "ij,bje->bie", earlier, hit.astype(jnp.bfloat16), preferred_element_type=jnp.float32
    )
    code = jnp.arange(blocks, dtype=jnp.int32)[:, None, None] * CAP + rank.astype(jnp.int32)
    code = jnp.where(hit, code, -1)
    flat = (blocks * block, exp_dev)
    return code.reshape(flat).T, gate_at.reshape(flat).T


def spread_body(
    queries,
    new_keys,
    new_values,
    cache_keys,
    cache_values,
    cache_lengths,
    residual,
    out_weight,
    norm_gain,
    expert_ids,
    gate_weights,
    w_gate,
    w_up,
    w_down,
):
    ctx_pos, tp_pos, req_pos = (lax.axis_index(a) for a in ("ctx", "tp", "req"))
    ctx_count, req_count = lax.axis_size("ctx"), lax.axis_size("req")
    tok_dev, heads, hd = queries.shape
    block, share = residual.shape
    exp_dev = w_gate.shape[0]
    slots = req_count * ctx_count * CAP
    length = lax.dynamic_index_in_dim(cache_lengths, req_pos, 0, keepdims=False)
    code, gate_at = route_tables(expert_ids, gate_weights, exp_dev)
    swap = [(a * ctx_count + b, b * ctx_count + a) for a in range(ctx_count) for b in range(ctx_count)]
    residual_t = lax.ppermute(residual, ("ctx", "tp"), swap)
    packs = attention_part(queries, new_keys, new_values, cache_keys, cache_values, length)
    packs = lax.all_to_all(packs, "ctx", 0, 0, tiled=True)
    attended = merge(packs, hd, heads)
    attended = lax.all_gather(attended, "ctx", tiled=True)
    part = jnp.dot(attended, out_weight, preferred_element_type=jnp.float32)
    part = part.reshape(-1, block, share)
    part = lax.all_to_all(part, "tp", 0, 0, tiled=True)
    hidden = jnp.sum(part, 0) + residual_t.astype(jnp.float32)
    squares = jnp.sum(hidden * hidden, 1)
    gain = lax.dynamic_slice_in_dim(norm_gain, ctx_pos * share, share, 0)
    scaled = (hidden * gain).astype(jnp.bfloat16)
    squares = lax.psum(squares, "ctx")
    factor = lax.rsqrt(squares / norm_gain.shape[0] + 1e-6)
    factor = lax.all_gather(factor, ("req", "tp"), tiled=True)
    scaled = lax.all_gather(scaled, ("req", "tp"), tiled=True)
    pick = code[:, None, :] == jnp.arange(slots, dtype=jnp.int32)[None, :, None]
    row_factor = jnp.sum(jnp.where(pick, factor, 0.0), -1, keepdims=True)
    row_gate = jnp.sum(jnp.where(pick, gate_at[:, None, :], 0.0), -1, keepdims=True)
    pick = pick.astype(jnp.bfloat16)
    rows = jnp.einsum("est,td->esd", pick, scaled, preferred_element_type=jnp.bfloat16)
    gate = jnp.einsum("esd,edf->esf", rows, w_gate, preferred_element_type=jnp.float32)
    up = jnp.einsum("esd,edf->esf", rows, w_up, preferred_element_type=jnp.float32)
    both = jnp.stack([gate, up], 2).astype(jnp.bfloat16)
    both = both.reshape(ctx_count, exp_dev * slots // ctx_count, 2, -1)
    both = lax.all_to_all(both, "ctx", 0, 0, tiled=True)
    both = both.astype(jnp.float32).sum(0)
    per = exp_dev * slots // ctx_count
    mine = lax.dynamic_slice_in_dim(row_factor.reshape(-1, 1), ctx_pos * per, per, 0)
    inner = (jax.nn.silu(both[:, 0] * mine) * (both[:, 1] * mine)).astype(jnp.bfloat16)
    inner = lax.all_gather(inner, "ctx", tiled=True).reshape(exp_dev, slots, -1)
    down = jnp.einsum("esf,efd->esd", inner, w_down, preferred_element_type=jnp.float32)
    down = (down * row_gate).astype(jnp.bfloat16)
    mixed = jnp.einsum("est,esd->td", pick, down, preferred_element_type=jnp.float32)
    mixed = mixed.astype(jnp.bfloat16).reshape(-1, block, share)
    mixed = lax.all_to_all(mixed, ("req", "tp"), 0, 0, tiled=True)
    out = hidden + jnp.sum(mixed.astype(jnp.float32), 0)
    return lax.ppermute(out.astype(jnp.bfloat16), ("ctx", "tp"), swap)


def body(*args):
    tokens = args[0].shape[0] * lax.axis_size("req")
    slots = args[11].shape[0] * lax.axis_size("req") * lax.axis_size("ctx") * CAP
    if tokens * slots * 2 <= FUSED_BYTES:
        return fused_body(*args)
    return spread_body(*args)


def solution(mesh):
    in_specs = (
        P("req", "tp", None),
        P("req", "tp", None),
        P("req", "tp", None),
        P("req", "ctx", "tp", None),
        P("req", "ctx", "tp", None),
        P(),
        P(("req", "ctx"), "tp"),
        P("tp", "ctx"),
        P(),
        P(("req", "ctx"), None),
        P(("req", "ctx"), None),
        P("req", "ctx", "tp"),
        P("req", "ctx", "tp"),
        P("req", "tp", "ctx"),
    )
    out_specs = P(("req", "ctx"), "tp")
    return jax.shard_map(body, mesh=mesh, in_specs=in_specs, out_specs=out_specs, check_vma=False)
```

```python
import functools
import jax
import jax.numpy as jnp
from jax import lax
from jax.experimental import pallas as pl
from jax.experimental.pallas import tpu as pltpu
from jax.sharding import PartitionSpec as P

TOP = 6
CAP = 8
MASKED = -1e30
F32 = jnp.float32
BF16 = jnp.bfloat16
CHUNKS = 4
FUSED_BYTES = 4 * 1024 * 1024


def dot(a, b, contract, kind=F32):
    return lax.dot_general(a, b, (contract, ((), ())), preferred_element_type=kind)


def layer_kernel(
    dims,
    len_ref,
    q_ref,
    ck_ref,
    cv_ref,
    nk_ref,
    nv_ref,
    res_ref,
    ow_ref,
    gain_ref,
    rt_ref,
    wg_hbm,
    wu_hbm,
    wd_hbm,
    out_ref,
    wg,
    wu,
    wd,
    pk_send,
    pk_recv,
    st_send,
    st_recv,
    att,
    part,
    part_recv,
    res_t,
    hidden,
    sq,
    fac,
    tab,
    codes,
    tok,
    pick,
    x,
    gu,
    r1,
    s2,
    r2,
    inner,
    ys,
    acc,
    mix,
    mix_recv,
    tsend,
    trecv,
    fin,
    fin_recv,
    w_sem,
    ssem,
    rsem,
):
    reqs, ctxs, tps, block, heads, hd, exp_dev, slots, ff, share = dims
    r, c, t = lax.axis_index("req"), lax.axis_index("ctx"), lax.axis_index("tp")
    blocks = reqs * ctxs
    tokens = blocks * block
    chunk = exp_dev * slots // CHUNKS
    quarter = chunk // ctxs
    rb = min(slots, quarter)
    y, k = c // 2, c % 2
    count = [0]

    def rcopy(src, dst, **where):
        i = count[0]
        count[0] = i + 1
        return pltpu.make_async_remote_copy(
            src_ref=src,
            dst_ref=dst,
            send_sem=ssem.at[i],
            recv_sem=rsem.at[i],
            device_id={"req": r, "ctx": c, "tp": t} | where,
            device_id_type=pl.DeviceIdType.MESH,
        )

    def step(me, d, n):
        return lax.rem(me + d, n)

    loads = [
        pltpu.make_async_copy(wg_hbm, wg, w_sem.at[0]),
        pltpu.make_async_copy(wu_hbm, wu, w_sem.at[1]),
        pltpu.make_async_copy(wd_hbm, wd, w_sem.at[2]),
    ]
    for load in loads:
        load.start()

    barrier = pltpu.get_barrier_semaphore()
    peers = [
        {"req": step(r, a, reqs), "ctx": step(c, b, ctxs), "tp": t}
        for a in range(reqs)
        for b in range(ctxs)
        if a or b
    ] + [{"req": r, "ctx": c, "tp": step(t, d, tps)} for d in range(1, tps)]
    swap = {"ctx": t, "tp": c}
    for peer in peers:
        pl.semaphore_signal(barrier, 1, device_id=peer, device_id_type=pl.DeviceIdType.MESH)

    @pl.when(c != t)
    def _():
        pl.semaphore_signal(
            barrier, 1, device_id={"req": r} | swap, device_id_type=pl.DeviceIdType.MESH
        )
        pl.semaphore_wait(barrier, len(peers) + 1)

    @pl.when(c == t)
    def _():
        pl.semaphore_wait(barrier, len(peers))

    pending = []

    me = r * ctxs + c
    tab_copies = []
    for a in range(reqs):
        for b in range(ctxs):
            if a or b:
                to = step(r, a, reqs)
                copy = rcopy(rt_ref.at[to], tab.at[me], req=to, ctx=step(c, b, ctxs))
                copy.start()
                tab_copies.append(copy)
    tab[me] = rt_ref[r]
    res_copy = rcopy(res_ref, res_t, **swap)

    @pl.when(c != t)
    def _():
        res_copy.start()

    @pl.when(c == t)
    def _():
        res_t[...] = res_ref[...]

    length = len_ref[r]
    cache_dev, new_dev = ck_ref.shape[0], nk_ref.shape[0]
    rows = heads * block
    scale = hd**-0.5
    old_at = lax.broadcasted_iota(jnp.int32, (cache_dev, rows), 0)
    old_ok = old_at < length - c * cache_dev
    new_at = lax.broadcasted_iota(jnp.int32, (new_dev, rows), 0)
    lane = lax.broadcasted_iota(jnp.int32, (new_dev, rows), 1) % block
    stat_at = lax.broadcasted_iota(jnp.int32, (8, rows), 0)
    last = jnp.where(c == ctxs - 1, 0, new_dev)
    pk_copies = []
    for d in list(range(1, ctxs)) + [0]:
        b = step(c, d, ctxs)
        q = q_ref[b]
        new_ok = new_at + last <= lane + b * block
        old = jnp.where(old_ok, dot(ck_ref[...], q, ((1,), (1,))) * scale, MASKED)
        new = jnp.where(new_ok, dot(nk_ref[...], q, ((1,), (1,))) * scale, MASKED)
        top = jnp.maximum(
            jnp.max(old, 0, keepdims=True), jnp.max(new, 0, keepdims=True)
        )
        old = jnp.where(old_ok, jnp.exp(old - top), 0.0)
        new = jnp.where(new_ok, jnp.exp(new - top), 0.0)
        total = jnp.sum(old, 0, keepdims=True) + jnp.sum(new, 0, keepdims=True)
        sums = dot(cv_ref[...], old.astype(BF16), ((0,), (0,)))
        sums = sums + dot(nv_ref[...], new.astype(BF16), ((0,), (0,)))
        pk_send[d] = sums.astype(BF16)
        st_send[d] = jnp.where(
            stat_at == 0, top, jnp.where(stat_at == 1, total, 0.0)
        )
        if d:
            for src, dst in ((pk_send, pk_recv), (st_send, st_recv)):
                copy = rcopy(src.at[d], dst.at[d], ctx=b)
                copy.start()
                pk_copies.append(copy)
    for copy in pk_copies:
        copy.wait_recv()
    pending += pk_copies
    packs = [pk_send[0]] + [pk_recv[d] for d in range(1, ctxs)]
    stats = [st_send[0]] + [st_recv[d] for d in range(1, ctxs)]
    tops = [st[0:1, :] for st in stats]
    top = functools.reduce(jnp.maximum, tops)
    total = jnp.zeros((1, rows), F32)
    sums = jnp.zeros((hd, rows), F32)
    for p, st, own in zip(packs, stats, tops):
        factor = jnp.exp(own - top)
        total = total + factor * st[1:2, :]
        sums = sums + factor * p.astype(F32)
    out = jnp.transpose(sums / total)
    for h in range(heads):
        att[c, :, h * hd : (h + 1) * hd] = out[h * block : (h + 1) * block].astype(BF16)
    att_copies = []
    for d in range(1, ctxs):
        copy = rcopy(att.at[c], att.at[c], ctx=step(c, d, ctxs))
        copy.start()
        att_copies.append(copy)
    for copy in tab_copies:
        copy.wait_recv()
    pending += tab_copies
    for p in range(blocks // 2):
        codes[:, p * 128 : (p + 1) * 128] = tab[2 * p] + tab[2 * p + 1]
    slot_at = lax.broadcasted_iota(jnp.int32, (rb, tokens), 0).astype(F32)

    def make_pick(i, carry):
        row = i * rb
        e = row // slots
        code = codes[pl.ds(e, 1), :] - (row - e * slots + 1).astype(F32)
        pick[pl.ds(pl.multiple_of(row, rb), rb), :] = jnp.where(
            slot_at == code, 1.0, 0.0
        ).astype(BF16)
        return carry

    lax.fori_loop(0, exp_dev * slots // rb, make_pick, 0)
    for copy in att_copies:
        copy.wait_recv()
    pending += att_copies
    width = heads * hd
    full = dot(att[...].reshape(ctxs * block, width), ow_ref[...], ((1,), (0,)))
    part[...] = full.reshape(tps, block, share).astype(BF16)
    part_copies = []
    for d in range(1, tps):
        to = step(t, d, tps)
        copy = rcopy(part.at[to], part_recv.at[d], tp=to)
        copy.start()
        part_copies.append(copy)
    hid = part[t].astype(F32)

    @pl.when(c != t)
    def _():
        res_copy.wait_recv()

    hid = hid + res_t[...].astype(F32)
    for d in range(1, tps):
        part_copies[d - 1].wait_recv()
        hid = hid + part_recv[d].astype(F32)
    pending += part_copies
    hidden[...] = hid
    tok[r * tps + t] = (hid * gain_ref[...]).astype(BF16)
    tok_copies = []
    for a in range(reqs):
        for d in range(tps):
            if (a == 0) and d:
                copy = rcopy(tok.at[r * tps + t], tok.at[r * tps + t], tp=step(t, d, tps))
                copy.start()
                tok_copies.append(copy)
    far_copies = []
    for a in range(1, reqs):
        copy = rcopy(tok.at[r * tps + t], tok.at[r * tps + t], req=step(r, a, reqs))
        copy.start()
        far_copies.append(copy)
    sq[0] = jnp.broadcast_to(jnp.sum(hid * hid, 1, keepdims=True), (block, 128))
    sq_copies = []
    for d in range(1, ctxs):
        copy = rcopy(sq.at[0], sq.at[d], ctx=step(c, d, ctxs))
        copy.start()
        sq_copies.append(copy)
    for copy in sq_copies:
        copy.wait_recv()
    pending += sq_copies
    squares = sq[0]
    for d in range(1, ctxs):
        squares = squares + sq[d]
    fac[r * tps + t] = lax.rsqrt(squares / (share * ctxs) + 1e-6)
    fac_copies = []
    for d in range(1, tps):
        copy = rcopy(fac.at[r * tps + t], fac.at[r * tps + t], tp=step(t, d, tps))
        copy.start()
        fac_copies.append(copy)
    fac_far = []
    for a in range(1, reqs):
        copy = rcopy(fac.at[r * tps + t], fac.at[r * tps + t], req=step(r, a, reqs))
        copy.start()
        fac_far.append(copy)
    for d in range(1, tps):
        tok_copies[d - 1].wait_recv()
        at = r * tps + step(t, tps - d, tps)
        for a in range(1, reqs):
            copy = rcopy(tok.at[at], tok.at[at], req=step(r, a, reqs))
            copy.start()
            far_copies.append(copy)
    for d in range(1, tps):
        fac_copies[d - 1].wait_recv()
        at = r * tps + step(t, tps - d, tps)
        for a in range(1, reqs):
            copy = rcopy(fac.at[at], fac.at[at], req=step(r, a, reqs))
            copy.start()
            fac_far.append(copy)
    for copy in far_copies:
        copy.wait_recv()
    pending += tok_copies + far_copies + fac_copies
    loads[0].wait()
    loads[1].wait()

    n_sub = chunk // rb
    n_q = quarter // rb
    first, second, third, fourth = [], [], [], []

    def up_stage(j):
        base = j * chunk
        x[...] = dot(
            pick[base : base + chunk, :], tok[...].reshape(tokens, share), ((1,), (0,))
        ).astype(BF16)

        def one(i, carry):
            e = (base + i * rb) // slots
            at = pl.ds(pl.multiple_of((i % n_q) * rb, rb), rb)
            xs = x[pl.ds(pl.multiple_of(i * rb, rb), rb), :]
            q = i // n_q
            gu[0, j, q // 2, q % 2, at, :] = dot(xs, wg[e], ((1,), (1,))).astype(BF16)
            gu[1, j, q // 2, q % 2, at, :] = dot(xs, wu[e], ((1,), (1,))).astype(BF16)
            return carry

        lax.fori_loop(0, n_sub, one, 0, unroll=min(4, n_sub))
        copy = rcopy(gu.at[:, j, :, 1 - k], r1.at[:, j], ctx=y * 2 + 1 - k)
        copy.start()
        first.append(copy)

    def pair_stage(j):
        first[j].wait_recv()
        s2[:, j] = (
            gu[:, j, 1 - y, k].astype(F32) + r1[:, j, 1 - y].astype(F32)
        ).astype(BF16)
        copy = rcopy(s2.at[:, j], r2.at[:, j], ctx=(1 - y) * 2 + k)
        copy.start()
        second.append(copy)

    def act_stage(j):
        second[j].wait_recv()
        both = gu[:, j, y, k].astype(F32) + r1[:, j, y].astype(F32) + r2[:, j].astype(F32)
        col = lax.broadcasted_iota(jnp.int32, (tokens, 128), 1)
        f = fac[...].reshape(tokens, 128)
        hi = f.astype(BF16).astype(F32)
        mid = (f - hi).astype(BF16).astype(F32)
        low = f - hi - mid
        f = jnp.where(col == 0, hi, jnp.where(col == 1, mid, jnp.where(col == 2, low, 0.0)))
        mine = pick[pl.ds(pl.multiple_of(j * chunk + c * quarter, quarter), quarter), :]
        row = jnp.sum(dot(mine, f.astype(BF16), ((1,), (0,))), 1, keepdims=True)
        g = both[0] * row
        inner[j, y, k] = (g * jax.nn.sigmoid(g) * (both[1] * row)).astype(BF16)
        copy = rcopy(inner.at[j, y, k], inner.at[j, y, k], ctx=(1 - y) * 2 + k)
        copy.start()
        third.append(copy)

    def share_stage(j):
        third[j].wait_recv()
        copy = rcopy(inner.at[j, :, k], inner.at[j, :, k], ctx=y * 2 + 1 - k)
        copy.start()
        fourth.append(copy)

    def down_stage(j):
        fourth[j].wait_recv()
        base = j * chunk

        def one(i, carry):
            e = (base + i * rb) // slots
            q = i // n_q
            at = pl.ds(pl.multiple_of((i % n_q) * rb, rb), rb)
            rows_at = pl.multiple_of(i * rb, rb)
            down = dot(inner[j, q // 2, q % 2, at, :], wd[e], ((1,), (0,)))
            mask = pick[pl.ds(pl.multiple_of(base + rows_at, rb), rb), :].astype(F32)
            gate = jnp.sum(mask * codes[pl.ds(exp_dev + e, 1), :], 1, keepdims=True)
            ys[pl.ds(rows_at, rb), :] = (down * gate).astype(BF16)
            return carry

        lax.fori_loop(0, n_sub, one, 0, unroll=min(4, n_sub))
        term = dot(pick[base : base + chunk, :], ys[...], ((0,), (0,)))
        if j == 0:
            acc[...] = term
        else:
            acc[...] += term

    up_stage(0)
    up_stage(1)
    pair_stage(0)
    up_stage(2)
    for copy in fac_far:
        copy.wait_recv()
    pending.extend(fac_far)
    act_stage(0)
    pair_stage(1)
    up_stage(3)
    loads[2].wait()
    share_stage(0)
    act_stage(1)
    pair_stage(2)
    down_stage(0)
    share_stage(1)
    act_stage(2)
    pair_stage(3)
    down_stage(1)
    share_stage(2)
    act_stage(3)
    down_stage(2)
    share_stage(3)
    down_stage(3)
    pending += first + second + third + fourth

    per = tps * block
    mix_copies = []
    for a in range(1, reqs):
        to = step(r, a, reqs)
        mix[a] = acc[pl.ds(pl.multiple_of(to * per, per), per), :].astype(BF16)
        copy = rcopy(mix.at[a], mix_recv.at[a], req=to)
        copy.start()
        mix_copies.append(copy)
    mixed = acc[pl.ds(pl.multiple_of(r * per, per), per), :]
    for a in range(1, reqs):
        mix_copies[a - 1].wait_recv()
        mixed = mixed + mix_recv[a].astype(F32)
    pending += mix_copies
    tsend[...] = mixed.reshape(tps, block, share).astype(BF16)
    t_copies = []
    for d in range(1, tps):
        to = step(t, d, tps)
        copy = rcopy(tsend.at[to], trecv.at[d], tp=to)
        copy.start()
        t_copies.append(copy)
    total = hidden[...] + tsend[t].astype(F32)
    for d in range(1, tps):
        t_copies[d - 1].wait_recv()
        total = total + trecv[d].astype(F32)
    pending += t_copies
    fin[...] = total.astype(BF16)
    fin_copy = rcopy(fin, fin_recv, **swap)

    @pl.when(c != t)
    def _():
        fin_copy.start()
        fin_copy.wait()
        res_copy.wait_send()
        out_ref[...] = fin_recv[...]

    @pl.when(c == t)
    def _():
        out_ref[...] = fin[...]

    for copy in pending:
        copy.wait_send()


def fused_body(
    queries,
    new_keys,
    new_values,
    cache_keys,
    cache_values,
    cache_lengths,
    residual,
    out_weight,
    norm_gain,
    expert_ids,
    gate_weights,
    w_gate,
    w_up,
    w_down,
):
    reqs, ctxs, tps = (lax.axis_size(a) for a in ("req", "ctx", "tp"))
    r, c = lax.axis_index("req"), lax.axis_index("ctx")
    tok_dev, heads, hd = queries.shape
    block, share = residual.shape
    exp_dev, _, ff = w_gate.shape
    blocks = reqs * ctxs
    slots = blocks * CAP
    tokens = blocks * block
    chunk = exp_dev * slots // CHUNKS
    quarter = chunk // ctxs
    rows = heads * block
    q = queries.reshape(ctxs, block, heads, hd).transpose(0, 2, 1, 3).reshape(ctxs, rows, hd)
    me = r * ctxs + c
    experts = jnp.arange(reqs * exp_dev, dtype=jnp.int32)
    hits = expert_ids[None, :, :] == experts[:, None, None]
    gates = jnp.sum(jnp.where(hits, gate_weights[None], 0.0), 2)
    hit = jnp.any(hits, 2)
    later = jnp.triu(jnp.ones((block, block), BF16), 0)
    rank = jnp.dot(hit.astype(BF16), later, preferred_element_type=F32)
    code = jnp.where(hit, rank + (me * CAP).astype(F32), 0.0)
    table = jnp.stack([code.reshape(reqs, exp_dev, block), gates.reshape(reqs, exp_dev, block)], 1)
    table = table.reshape(reqs, 2 * exp_dev, block)
    zero = jnp.zeros_like(table)
    odd = me % 2 == 1
    table = jnp.concatenate([jnp.where(odd, zero, table), jnp.where(odd, table, zero)], 2)
    gain = lax.dynamic_slice_in_dim(norm_gain, c * share, share, 0).reshape(1, share)
    dims = (reqs, ctxs, tps, block, heads, hd, exp_dev, slots, ff, share)
    n_rem = (
        (blocks - 1)
        + 2
        + 3 * (ctxs - 1)
        + (tps - 1)
        + (ctxs - 1)
        + 2 * (tps - 1)
        + 2 * tps * (reqs - 1)
        + 4 * CHUNKS
        + (reqs - 1)
        + (tps - 1)
    )
    vmem = pl.BlockSpec(memory_space=pltpu.VMEM)
    anywhere = pl.BlockSpec(memory_space=pl.ANY)
    scratch = [
        ((exp_dev, ff, share), BF16),
        ((exp_dev, ff, share), BF16),
        ((exp_dev, ff, share), BF16),
        ((ctxs, hd, rows), BF16),
        ((ctxs, hd, rows), BF16),
        ((ctxs, 8, rows), F32),
        ((ctxs, 8, rows), F32),
        ((ctxs, block, heads * hd), BF16),
        ((tps, block, share), BF16),
        ((tps, block, share), BF16),
        ((block, share), BF16),
        ((block, share), F32),
        ((ctxs, block, 128), F32),
        ((reqs * tps, block, 128), F32),
        ((blocks, 2 * exp_dev, 128), F32),
        ((2 * exp_dev, tokens), F32),
        ((reqs * tps, block, share), BF16),
        ((exp_dev * slots, tokens), BF16),
        ((chunk, share), BF16),
        ((2, CHUNKS, 2, 2, quarter, ff), BF16),
        ((2, CHUNKS, 2, quarter, ff), BF16),
        ((2, CHUNKS, quarter, ff), BF16),
        ((2, CHUNKS, quarter, ff), BF16),
        ((CHUNKS, 2, 2, quarter, ff), BF16),
        ((chunk, share), BF16),
        ((tokens, share), F32),
        ((reqs, tps * block, share), BF16),
        ((reqs, tps * block, share), BF16),
        ((tps, block, share), BF16),
        ((tps, block, share), BF16),
        ((block, share), BF16),
        ((block, share), BF16),
    ]
    return pl.pallas_call(
        functools.partial(layer_kernel, dims),
        out_shape=jax.ShapeDtypeStruct((block, share), BF16),
        in_specs=[pl.BlockSpec(memory_space=pltpu.SMEM)] + [vmem] * 9 + [anywhere] * 3,
        out_specs=vmem,
        scratch_shapes=[pltpu.VMEM(*s) for s in scratch]
        + [
            pltpu.SemaphoreType.DMA((3,)),
            pltpu.SemaphoreType.DMA((n_rem,)),
            pltpu.SemaphoreType.DMA((n_rem,)),
        ],
        compiler_params=pltpu.CompilerParams(
            collective_id=0, has_side_effects=True, vmem_limit_bytes=63 * 1024 * 1024
        ),
    )(
        cache_lengths,
        q,
        cache_keys[0, :, 0, :],
        cache_values[0, :, 0, :],
        new_keys[:, 0, :],
        new_values[:, 0, :],
        residual,
        out_weight,
        gain,
        table,
        jnp.swapaxes(w_gate, 1, 2),
        jnp.swapaxes(w_up, 1, 2),
        w_down,
    )


def attention_part(queries, new_keys, new_values, cache_keys, cache_values, length):
    ctx_pos, ctx_count = lax.axis_index("ctx"), lax.axis_size("ctx")
    tok_dev, heads, hd = queries.shape
    cache_dev = cache_keys.shape[1]
    block = tok_dev // ctx_count
    rows = heads * block
    q = queries.reshape(ctx_count, block, heads, hd).transpose(0, 2, 1, 3)
    q = q.reshape(ctx_count * rows, hd)
    keys = jnp.concatenate([cache_keys[0, :, 0, :], new_keys[:, 0, :]], 0)
    values = jnp.concatenate([cache_values[0, :, 0, :], new_values[:, 0, :]], 0)
    scores = jnp.dot(keys, q.T, preferred_element_type=jnp.float32) * (hd**-0.5)
    key_at = jnp.arange(cache_dev + tok_dev, dtype=jnp.int32)[:, None]
    row_at = jnp.arange(ctx_count * rows, dtype=jnp.int32)[None, :]
    token = (row_at // rows) * block + row_at % block
    valid = jnp.where(
        key_at < cache_dev,
        ctx_pos * cache_dev + key_at < length,
        jnp.logical_and(ctx_pos == ctx_count - 1, key_at - cache_dev <= token),
    )
    scores = jnp.where(valid, scores, MASKED)
    top = jnp.max(scores, 0, keepdims=True)
    weights = jnp.where(valid, jnp.exp(scores - top), 0.0)
    total = jnp.sum(weights, 0, keepdims=True)
    sums = lax.dot_general(
        values,
        weights.astype(jnp.bfloat16),
        (((0,), (0,)), ((), ())),
        preferred_element_type=jnp.float32,
    )
    pack = jnp.concatenate([sums, top, total, jnp.zeros((6, ctx_count * rows), jnp.float32)], 0)
    return pack.reshape(hd + 8, ctx_count, rows).transpose(1, 0, 2)


def merge(packs, hd, heads):
    top = jnp.max(packs[:, hd : hd + 1], 0)
    factor = jnp.exp(packs[:, hd : hd + 1] - top)
    total = jnp.sum(factor * packs[:, hd + 1 : hd + 2], 0)
    out = (jnp.sum(factor * packs[:, :hd], 0) / total).astype(jnp.bfloat16)
    block = out.shape[1] // heads
    return out.reshape(hd, heads, block).transpose(2, 1, 0).reshape(block, heads * hd)


def route_tables(expert_ids, gate_weights, exp_dev):
    block = expert_ids.shape[0]
    both = jnp.concatenate([expert_ids.astype(jnp.float32), gate_weights], 1)
    both = lax.all_gather(both, ("req", "ctx"))
    blocks = both.shape[0]
    ids = both[:, :, :TOP].astype(jnp.int32)
    gates = both[:, :, TOP:]
    first = lax.axis_index("req") * exp_dev
    experts = first + jnp.arange(exp_dev, dtype=jnp.int32)
    hits = ids[:, :, :, None] == experts
    gate_at = jnp.sum(jnp.where(hits, gates[..., None], 0.0), 2)
    hit = jnp.any(hits, 2)
    earlier = jnp.tril(jnp.ones((block, block), jnp.bfloat16), -1)
    rank = jnp.einsum(
        "ij,bje->bie", earlier, hit.astype(jnp.bfloat16), preferred_element_type=jnp.float32
    )
    code = jnp.arange(blocks, dtype=jnp.int32)[:, None, None] * CAP + rank.astype(jnp.int32)
    code = jnp.where(hit, code, -1)
    flat = (blocks * block, exp_dev)
    return code.reshape(flat).T, gate_at.reshape(flat).T


def spread_body(
    queries,
    new_keys,
    new_values,
    cache_keys,
    cache_values,
    cache_lengths,
    residual,
    out_weight,
    norm_gain,
    expert_ids,
    gate_weights,
    w_gate,
    w_up,
    w_down,
):
    ctx_pos, tp_pos, req_pos = (lax.axis_index(a) for a in ("ctx", "tp", "req"))
    ctx_count, req_count = lax.axis_size("ctx"), lax.axis_size("req")
    tok_dev, heads, hd = queries.shape
    block, share = residual.shape
    exp_dev = w_gate.shape[0]
    slots = req_count * ctx_count * CAP
    length = lax.dynamic_index_in_dim(cache_lengths, req_pos, 0, keepdims=False)
    code, gate_at = route_tables(expert_ids, gate_weights, exp_dev)
    swap = [(a * ctx_count + b, b * ctx_count + a) for a in range(ctx_count) for b in range(ctx_count)]
    residual_t = lax.ppermute(residual, ("ctx", "tp"), swap)
    packs = attention_part(queries, new_keys, new_values, cache_keys, cache_values, length)
    packs = lax.all_to_all(packs, "ctx", 0, 0, tiled=True)
    attended = merge(packs, hd, heads)
    attended = lax.all_gather(attended, "ctx", tiled=True)
    part = jnp.dot(attended, out_weight, preferred_element_type=jnp.float32)
    part = part.reshape(-1, block, share)
    part = lax.all_to_all(part, "tp", 0, 0, tiled=True)
    hidden = jnp.sum(part, 0) + residual_t.astype(jnp.float32)
    squares = jnp.sum(hidden * hidden, 1)
    gain = lax.dynamic_slice_in_dim(norm_gain, ctx_pos * share, share, 0)
    scaled = (hidden * gain).astype(jnp.bfloat16)
    squares = lax.psum(squares, "ctx")
    factor = lax.rsqrt(squares / norm_gain.shape[0] + 1e-6)
    factor = lax.all_gather(factor, ("req", "tp"), tiled=True)
    scaled = lax.all_gather(scaled, ("req", "tp"), tiled=True)
    pick = code[:, None, :] == jnp.arange(slots, dtype=jnp.int32)[None, :, None]
    row_factor = jnp.sum(jnp.where(pick, factor, 0.0), -1, keepdims=True)
    row_gate = jnp.sum(jnp.where(pick, gate_at[:, None, :], 0.0), -1, keepdims=True)
    pick = pick.astype(jnp.bfloat16)
    rows = jnp.einsum("est,td->esd", pick, scaled, preferred_element_type=jnp.bfloat16)
    gate = jnp.einsum("esd,edf->esf", rows, w_gate, preferred_element_type=jnp.float32)
    up = jnp.einsum("esd,edf->esf", rows, w_up, preferred_element_type=jnp.float32)
    both = jnp.stack([gate, up], 2).astype(jnp.bfloat16)
    both = both.reshape(ctx_count, exp_dev * slots // ctx_count, 2, -1)
    both = lax.all_to_all(both, "ctx", 0, 0, tiled=True)
    both = both.astype(jnp.float32).sum(0)
    per = exp_dev * slots // ctx_count
    mine = lax.dynamic_slice_in_dim(row_factor.reshape(-1, 1), ctx_pos * per, per, 0)
    inner = (jax.nn.silu(both[:, 0] * mine) * (both[:, 1] * mine)).astype(jnp.bfloat16)
    inner = lax.all_gather(inner, "ctx", tiled=True).reshape(exp_dev, slots, -1)
    down = jnp.einsum("esf,efd->esd", inner, w_down, preferred_element_type=jnp.float32)
    down = (down * row_gate).astype(jnp.bfloat16)
    mixed = jnp.einsum("est,esd->td", pick, down, preferred_element_type=jnp.float32)
    mixed = mixed.astype(jnp.bfloat16).reshape(-1, block, share)
    mixed = lax.all_to_all(mixed, ("req", "tp"), 0, 0, tiled=True)
    out = hidden + jnp.sum(mixed.astype(jnp.float32), 0)
    return lax.ppermute(out.astype(jnp.bfloat16), ("ctx", "tp"), swap)


def body(*args):
    tokens = args[0].shape[0] * lax.axis_size("req")
    slots = args[11].shape[0] * lax.axis_size("req") * lax.axis_size("ctx") * CAP
    if tokens * slots * 2 <= FUSED_BYTES:
        return fused_body(*args)
    return spread_body(*args)


def solution(mesh):
    in_specs = (
        P("req", "tp", None),
        P("req", "tp", None),
        P("req", "tp", None),
        P("req", "ctx", "tp", None),
        P("req", "ctx", "tp", None),
        P(),
        P(("req", "ctx"), "tp"),
        P("tp", "ctx"),
        P(),
        P(("req", "ctx"), None),
        P(("req", "ctx"), None),
        P("req", "ctx", "tp"),
        P("req", "ctx", "tp"),
        P("req", "tp", "ctx"),
    )
    out_specs = P(("req", "ctx"), "tp")
    return jax.shard_map(body, mesh=mesh, in_specs=in_specs, out_specs=out_specs, check_vma=False)
```
